32 devices in a mesh: fsdp: 4 (over x, core), ctx: 4 (over z), tp: 2 (over y).
Axes of the slice: x: 2, y: 2, z: 4, core: 2. Of those that a mesh axis runs over, the one named last changes fastest.
Arguments:
- hidden_in: bfloat16 [4, 512, 768], P('fsdp', 'ctx'), may hold values from -6 to 6
- cotangent: bfloat16 [4, 512, 768], P('fsdp', 'ctx'), may hold values from -6 to 6
- segments: int32 [4, 512], P('fsdp'), may hold values from 0 to 3, never falling along the last dimension, each value on 1 to 256 neighbouring positions
- attn_gain: bfloat16 [2, 768], P(None, 'fsdp'), may hold values from 0.099609375 to 1.8984375
- attn_shift: bfloat16 [2, 768], P(None, 'fsdp'), may hold values from -4 to 4
- qkv_weight: bfloat16 [2, 3, 768, 768], P(None, None, 'fsdp', 'tp'), may hold values from -0.21875 to 0.21875
- qkv_bias: bfloat16 [2, 3, 768], P(None, None, ('tp', 'fsdp')), may hold values from -4 to 4
- dense_weight: bfloat16 [2, 768, 768], P(None, 'tp', 'fsdp'), may hold values from -1.75 to 1.75
- dense_bias: bfloat16 [2, 768], P(None, 'fsdp'), may hold values from -3 to 3
- mlp_gain: bfloat16 [2, 768], P(None, 'fsdp'), may hold values from 0.099609375 to 1.8984375
- mlp_shift: bfloat16 [2, 768], P(None, 'fsdp'), may hold values from -4 to 4
- up_weight: bfloat16 [2, 768, 3072], P(None, 'fsdp', 'tp'), may hold values from -0.21875 to 0.21875
- up_bias: bfloat16 [2, 3072], P(None, ('tp', 'fsdp')), may hold values from -4 to 4
- down_weight: bfloat16 [2, 3072, 768], P(None, 'tp', 'fsdp'), may hold values from -0.109375 to 0.109375
- down_bias: bfloat16 [2, 768], P(None, 'fsdp'), may hold values from -3 to 3
Outputs:
- hidden_out: bfloat16 [4, 512, 768], P('fsdp', 'ctx')
- grad_input: float32 [4, 512, 768], P('fsdp', 'ctx')
- grad_attn_gain: float32 [2, 768], P(None, 'fsdp')
- grad_attn_shift: float32 [2, 768], P(None, 'fsdp')
- grad_qkv_weight: float32 [2, 3, 768, 768], P(None, None, 'fsdp', 'tp')
- grad_qkv_bias: float32 [2, 3, 768], P(None, None, ('tp', 'fsdp'))
- grad_dense_weight: float32 [2, 768, 768], P(None, 'tp', 'fsdp')
- grad_dense_bias: float32 [2, 768], P(None, 'fsdp')
- grad_mlp_gain: float32 [2, 768], P(None, 'fsdp')
- grad_mlp_shift: float32 [2, 768], P(None, 'fsdp')
- grad_up_weight: float32 [2, 768, 3072], P(None, 'fsdp', 'tp')
- grad_up_bias: float32 [2, 3072], P(None, ('tp', 'fsdp'))
- grad_down_weight: float32 [2, 3072, 768], P(None, 'tp', 'fsdp')
- grad_down_bias: float32 [2, 768], P(None, 'fsdp')
The draws below stay inside these ranges and needn't reach their ends.
Inputs may be any that keep to these rules, and one draw needn't show every extreme that they name: `segments`: within a pack the numbers never fall; no document is longer than 256 positions.
All inputs are finite; a program needn't handle non-finite values.
Results may differ from the reference program's by a relative error of at most 0.03.
Values may be sent and summed in bfloat16 or wider, within the bound.
No kernel may reach another device: no remote copies, remote signals or barrier semaphores. Data moves between devices by JAX's collectives and lax.ppermute only.
A program may use at most 192 MiB of HBM per device.

```python
import math
import jax
import jax.numpy as jnp
import numpy as np
from jax import lax

D = 768
HD = 64
FF = 3072
ROT = 16
LAYERS = 2
SEGS = 4
SEQ = 512
PACKS = 4


def levels(key, shape, cuts, least, high):
    loudness = 1.0
    for position, shards_of in cuts:
        draws = jax.random.uniform(jax.random.fold_in(jax.random.fold_in(key, 6), position), (shards_of,), jnp.float32, least / len(cuts), high / len(cuts))
        loudness = loudness * jnp.repeat(jnp.exp(draws), shape[position] // shards_of).reshape((-1,) + (1,) * (len(shape) - 1 - position))
    return loudness


def split_up(count, total, most, skew):
    loads = [(1 << 20) // math.isqrt(grade ** skew) + 1 for grade in range(2, count + 1)]
    surplus, counts = total - most - (count - 1), [1] * (count - 1)
    while surplus > 0:
        candidates = [i for i in range(count - 1) if counts[i] < most]
        pool, budget = sum([loads[i] for i in candidates]), surplus
        for i in candidates:
            extra = min(most - counts[i], max(1, budget * loads[i] // pool), surplus)
            counts[i] = counts[i] + extra
            surplus = surplus - extra
    return np.array([most] + counts)


def ragged(stream_key, amount, total, reach, slope):
    if amount == 2:
        one = jax.random.randint(stream_key, (), max(1, total - reach), min(reach, total - 1) + 1)
        return jnp.stack([one, total - one])
    lengths = jnp.asarray(split_up(amount, total, reach, slope), jnp.int32)
    pairs = (amount - 1) // 2
    source_of, sink = lengths[1:1 + 2 * pairs:2], lengths[2:2 + 2 * pairs:2]
    margin = jnp.minimum(source_of - 1, reach - sink)
    shifted = jax.random.randint(jax.random.fold_in(stream_key, 1), (pairs,), 0, 1 << 20) % (margin + 1)
    lengths = lengths.at[1:1 + 2 * pairs:2].set(source_of - shifted).at[2:2 + 2 * pairs:2].set(sink + shifted)
    return lengths[jax.random.permutation(jax.random.fold_in(stream_key, 2), amount)]


def bell_draw(own_key, dims, width, limit, cuts=(), dtype=jnp.bfloat16):
    values = width * jax.random.normal(own_key, dims, jnp.float32)
    if cuts:
        values = values * levels(own_key, dims, cuts, -0.22, 0.18)
    return jnp.clip(values, -limit, limit).astype(dtype)


def setup_inputs(seed: int = 0) -> dict:
    seeds = jax.random.split(jax.random.key(seed), 16)
    return {
        "hidden_in": bell_draw(seeds[0], (PACKS, SEQ, D), 1.0, 6.0, ((0, 4), (1, 4))),
        "cotangent": bell_draw(seeds[1], (PACKS, SEQ, D), 1.0, 6.0, ((0, 4), (1, 4))),
        "segments": jax.vmap(lambda own: jnp.searchsorted(jnp.cumsum(ragged(own, SEGS, SEQ, SEQ // 2, 1)), jnp.arange(SEQ), side="right"))(jax.random.split(seeds[2], PACKS)).reshape((PACKS, SEQ)).astype(jnp.int32),
        "attn_gain": jnp.clip(1.0 + 0.18 * jax.random.normal(seeds[3], (LAYERS, D), jnp.float32), 0.099609375, 1.8984375).astype(jnp.bfloat16),
        "attn_shift": bell_draw(seeds[4], (LAYERS, D), 0.8, 4.0, ((1, 4),)),
        "qkv_weight": bell_draw(seeds[5], (LAYERS, 3, D, D), D ** -0.5, 0.21875, ((2, 4), (3, 2))),
        "qkv_bias": bell_draw(seeds[6], (LAYERS, 3, D), 1.0, 4.0, ((2, 8),)),
        "dense_weight": bell_draw(seeds[7], (LAYERS, D, D), (D // 64) ** -0.5, 1.75, ((1, 2), (2, 4))),
        "dense_bias": bell_draw(seeds[8], (LAYERS, D), 0.5, 3.0, ((1, 4),)),
        "mlp_gain": jnp.clip(1.0 + 0.18 * jax.random.normal(seeds[9], (LAYERS, D), jnp.float32), 0.099609375, 1.8984375).astype(jnp.bfloat16),
        "mlp_shift": bell_draw(seeds[10], (LAYERS, D), 0.8, 4.0, ((1, 4),)),
        "up_weight": bell_draw(seeds[11], (LAYERS, D, FF), D ** -0.5, 0.21875, ((1, 4), (2, 2))),
        "up_bias": bell_draw(seeds[12], (LAYERS, FF), 0.8, 4.0, ((1, 8),)),
        "down_weight": bell_draw(seeds[13], (LAYERS, FF, D), FF ** -0.5, 0.109375, ((1, 2), (2, 4))),
        "down_bias": bell_draw(seeds[14], (LAYERS, D), 0.5, 3.0, ((1, 4),)),
    }


EPSILON = 1e-05
MASKED = -1e+30

def rotary_tables(positions):
    halfway = ROT // 2
    frequency = jnp.exp(jnp.arange(halfway).astype(jnp.float32) * (-2.0 * math.log(10000.0) / ROT))
    angles = positions[:, None] * frequency[None, :]
    return (jnp.cos(angles), jnp.sin(angles))

def rotate(blocks, cosine_table, sine_table, direction):
    halfway = ROT // 2
    first_half = blocks[..., :halfway]
    second_half = blocks[..., halfway:ROT]
    cosine_rows = cosine_table[:, None, :]
    sine_rows = sine_table[:, None, :] * direction
    return jnp.concatenate([first_half * cosine_rows - second_half * sine_rows, second_half * cosine_rows + first_half * sine_rows, blocks[..., ROT:]], axis=-1)

def normalize(inputs, scales, shifts):
    center = inputs - lax.optimization_barrier(jnp.mean(inputs, axis=-1, keepdims=True))
    inverse = lax.rsqrt(lax.optimization_barrier(jnp.mean(center * center, axis=-1, keepdims=True)) + EPSILON)
    unit_vals = center * inverse
    return (unit_vals * scales.astype(jnp.float32) + shifts.astype(jnp.float32), unit_vals, inverse)

def normalize_back(incoming, unit_vals, inverse, scales):
    scaled = incoming * scales.astype(jnp.float32)
    inner = scaled - lax.optimization_barrier(jnp.mean(scaled, axis=-1, keepdims=True)) - unit_vals * lax.optimization_barrier(jnp.mean(scaled * unit_vals, axis=-1, keepdims=True))
    return (inverse * inner, lax.optimization_barrier(jnp.sum(incoming * unit_vals, axis=0)), lax.optimization_barrier(jnp.sum(incoming, axis=0)))

def gelu_pair(inputs):
    normal_cdf = 0.5 * (1.0 + lax.erf(inputs * (1.0 / math.sqrt(2.0))))
    density = jnp.exp(-0.5 * inputs * inputs) * (1.0 / math.sqrt(2.0 * math.pi))
    return (inputs * normal_cdf, normal_cdf + inputs * density)

def attention_scores(queries, key_heads, allowed):
    scores = jnp.einsum('qhd,khd->hqk', queries.astype(jnp.float32), key_heads.astype(jnp.float32)) * (1.0 / math.sqrt(HD))
    scores = jnp.where(allowed[None, :, :], scores, MASKED)
    peak_score = lax.optimization_barrier(jnp.max(scores, axis=-1, keepdims=True))
    log_total = peak_score[..., 0] + jnp.log(lax.optimization_barrier(jnp.sum(jnp.exp(scores - peak_score), axis=-1)))
    return (scores, log_total)

def layer_forward(hidden, weights, allowed, cosine_table, sine_table):
    attn_gain, attn_shift, qkv_weight, qkv_bias, dense_weight, dense_bias, mlp_gain, mlp_shift, up_weight, up_bias, down_weight, down_bias = weights
    row_count = hidden.shape[0]
    feature_width = qkv_weight.shape[2]
    head_count = feature_width // HD
    normed, unit_attn, inverse_attn = normalize(hidden, attn_gain, attn_shift)
    attn_in = normed.astype(jnp.bfloat16)

    def project(member):
        raw_rows = jnp.dot(attn_in, qkv_weight[member], preferred_element_type=jnp.float32) + qkv_bias[member].astype(jnp.float32)
        return raw_rows.reshape(row_count, head_count, HD)
    queries = rotate(project(0), cosine_table, sine_table, 1.0).astype(jnp.bfloat16)
    key_heads = rotate(project(1), cosine_table, sine_table, 1.0).astype(jnp.bfloat16)
    value_heads = project(2).astype(jnp.bfloat16)
    scores, log_total = attention_scores(queries, key_heads, allowed)
    probs_low = jnp.exp(scores - log_total[:, :, None]).astype(jnp.bfloat16)
    attended = jnp.einsum('hqk,khd->qhd', probs_low.astype(jnp.float32), value_heads.astype(jnp.float32))
    attended = attended.astype(jnp.bfloat16).reshape(row_count, feature_width)
    attn_out = jnp.dot(attended, dense_weight, preferred_element_type=jnp.float32)
    normed_mlp, unit_mlp, inverse_mlp = normalize(hidden, mlp_gain, mlp_shift)
    mlp_in = normed_mlp.astype(jnp.bfloat16)
    pre_act = jnp.dot(mlp_in, up_weight, preferred_element_type=jnp.float32) + up_bias.astype(jnp.float32)
    activated, slopes = gelu_pair(pre_act)
    act_low = activated.astype(jnp.bfloat16)
    mlp_out = jnp.dot(act_low, down_weight, preferred_element_type=jnp.float32)
    result = hidden + attn_out + mlp_out + dense_bias.astype(jnp.float32) + down_bias.astype(jnp.float32)
    stored = (attn_in, unit_attn, inverse_attn, mlp_in, unit_mlp, inverse_mlp, queries, key_heads, value_heads, log_total, attended, slopes, act_low)
    return (result, stored)

def layer_backward(upstream, weights, stored, allowed, cosine_table, sine_table):
    attn_gain, attn_shift, qkv_weight, qkv_bias, dense_weight, dense_bias, mlp_gain, mlp_shift, up_weight, up_bias, down_weight, down_bias = weights
    attn_in, unit_attn, inverse_attn, mlp_in, unit_mlp, inverse_mlp, queries, key_heads, value_heads, log_total, attended, slopes, act_low = stored
    row_count = upstream.shape[0]
    feature_width = qkv_weight.shape[2]
    head_count = feature_width // HD
    upstream_low = upstream.astype(jnp.bfloat16)
    grad_out_bias = lax.optimization_barrier(jnp.sum(upstream, axis=0))
    grad_down_weight = jnp.dot(act_low.T, upstream_low, preferred_element_type=jnp.float32)
    grad_pre = jnp.dot(upstream_low, down_weight.T, preferred_element_type=jnp.float32) * slopes
    grad_pre_low = grad_pre.astype(jnp.bfloat16)
    grad_up_weight = jnp.dot(mlp_in.T, grad_pre_low, preferred_element_type=jnp.float32)
    grad_up_bias = lax.optimization_barrier(jnp.sum(grad_pre, axis=0))
    into_mlp = jnp.dot(grad_pre_low, up_weight.T, preferred_element_type=jnp.float32)
    grad_dense_weight = jnp.dot(attended.T, upstream_low, preferred_element_type=jnp.float32)
    grad_att = jnp.dot(upstream_low, dense_weight.T, preferred_element_type=jnp.float32).astype(jnp.bfloat16)
    grad_att = grad_att.reshape(row_count, head_count, HD).astype(jnp.float32)
    attended_heads = attended.reshape(row_count, head_count, HD).astype(jnp.float32)
    row_delta = jnp.einsum('qhd,qhd->hq', grad_att, attended_heads)
    scores, unused_total = attention_scores(queries, key_heads, allowed)
    probs = jnp.exp(scores - log_total[:, :, None])
    grad_prob = jnp.einsum('qhd,khd->hqk', grad_att, value_heads.astype(jnp.float32))
    grad_score = (probs * (grad_prob - row_delta[:, :, None])).astype(jnp.bfloat16).astype(jnp.float32)
    inv_root = 1.0 / math.sqrt(HD)
    grad_query = jnp.einsum('hqk,khd->qhd', grad_score, key_heads.astype(jnp.float32)) * inv_root
    grad_key = jnp.einsum('hqk,qhd->khd', grad_score, queries.astype(jnp.float32)) * inv_root
    grad_value = jnp.einsum('hqk,qhd->khd', probs.astype(jnp.bfloat16).astype(jnp.float32), grad_att)
    grad_query = rotate(grad_query, cosine_table, sine_table, -1.0).reshape(row_count, feature_width)
    grad_key = rotate(grad_key, cosine_table, sine_table, -1.0).reshape(row_count, feature_width)
    grad_value = grad_value.reshape(row_count, feature_width)
    pieces = (grad_query, grad_key, grad_value)
    low_pieces = [piece.astype(jnp.bfloat16) for piece in pieces]
    grad_qkv_weight = jnp.stack([jnp.dot(attn_in.T, piece, preferred_element_type=jnp.float32) for piece in low_pieces])
    grad_qkv_bias = jnp.stack([lax.optimization_barrier(jnp.sum(piece, axis=0)) for piece in pieces])
    into_attn = jnp.dot(low_pieces[0], qkv_weight[0].T, preferred_element_type=jnp.float32)
    into_attn = into_attn + jnp.dot(low_pieces[1], qkv_weight[1].T, preferred_element_type=jnp.float32)
    into_attn = into_attn + jnp.dot(low_pieces[2], qkv_weight[2].T, preferred_element_type=jnp.float32)
    back_attn, grad_attn_gain, grad_attn_shift = normalize_back(into_attn, unit_attn, inverse_attn, attn_gain)
    back_mlp, grad_mlp_gain, grad_mlp_shift = normalize_back(into_mlp, unit_mlp, inverse_mlp, mlp_gain)
    lower_grad = upstream + back_attn + back_mlp
    grads = (grad_attn_gain, grad_attn_shift, grad_qkv_weight, grad_qkv_bias, grad_dense_weight, grad_out_bias, grad_mlp_gain, grad_mlp_shift, grad_up_weight, grad_up_bias, grad_down_weight, grad_out_bias)
    return (lower_grad, grads)

def reference(hidden_in, cotangent, segments, attn_gain, attn_shift, qkv_weight, qkv_bias, dense_weight, dense_bias, mlp_gain, mlp_shift, up_weight, up_bias, down_weight, down_bias):
    params = (attn_gain, attn_shift, qkv_weight, qkv_bias, dense_weight, dense_bias, mlp_gain, mlp_shift, up_weight, up_bias, down_weight, down_bias)
    positions = jnp.arange(SEQ).astype(jnp.float32)
    cosine_table, sine_table = rotary_tables(positions)
    index_row = jnp.arange(SEQ).astype(jnp.int32)
    causal = index_row[None, :] <= index_row[:, None]

    def one_pack(totals, packed):
        inputs, upstream_in, seg_row = packed
        allowed = causal & (seg_row[:, None] == seg_row[None, :])
        hidden = inputs.astype(jnp.float32)
        stored_all = []
        for which_layer in range(LAYERS):
            layer_params = tuple((tensor[which_layer] for tensor in params))
            hidden, stored = layer_forward(hidden, layer_params, allowed, cosine_table, sine_table)
            stored_all.append(stored)
        upstream = upstream_in.astype(jnp.float32)
        layer_grads = [None] * LAYERS
        for which_layer in reversed(range(LAYERS)):
            layer_params = tuple((tensor[which_layer] for tensor in params))
            upstream, layer_grads[which_layer] = layer_backward(upstream, layer_params, stored_all[which_layer], allowed, cosine_table, sine_table)
        stacked = tuple((jnp.stack([layer_grads[which][member] for which in range(LAYERS)]) for member in range(12)))
        totals = tuple((running + addend for running, addend in zip(totals, stacked)))
        return (totals, (hidden.astype(jnp.bfloat16), upstream))
    zero_grads = tuple((jnp.zeros(tensor.shape, jnp.float32) for tensor in params))
    totals, (hidden_out, grad_input) = lax.scan(one_pack, zero_grads, (hidden_in, cotangent, segments))
    return (hidden_out, grad_input, totals[0], totals[1], totals[2], totals[3], totals[4], totals[5], totals[6], totals[7], totals[8], totals[9], totals[10], totals[11])
```

```python
import math

import jax
import jax.numpy as jnp
from jax import lax
from jax.sharding import PartitionSpec as P

HD = 64
ROT = 16
LAYERS = 2
EPSILON = 1e-05
MASKED = -1e30
BF = jnp.bfloat16
F32 = jnp.float32


def flip(x, axis, bits, count):
    return lax.ppermute(x, axis, [(i, i ^ bits) for i in range(count)])


def tp_swap(x):
    return flip(x, "tp", 1, 2)


def pair_swap(x):
    return flip(x, "ctx", 1, 4)


def dot(a, b, dims):
    return lax.dot_general(a, b, (dims, ((), ())), preferred_element_type=F32)


def gather_rows(x, n):
    if n != 4:
        return lax.all_gather(x, "fsdp", axis=0, tiled=True)
    both = jnp.concatenate([x, flip(x, "fsdp", 2, n)], axis=0)
    return jnp.concatenate([both, flip(both, "fsdp", 1, n)], axis=0)


def scatter_rows(x, n):
    if n != 4:
        return lax.psum_scatter(x, "fsdp", scatter_dimension=0, tiled=True)
    half = x.shape[0] // 2
    x = x[:half] + flip(x[half:].astype(BF), "fsdp", 1, n).astype(F32)
    half = half // 2
    return x[:half] + flip(x[half:].astype(BF), "fsdp", 2, n).astype(F32)


def scatter_columns(x, n):
    if n != 4:
        return lax.psum_scatter(x, "fsdp", scatter_dimension=1, tiled=True)
    half = x.shape[1] // 2
    x = x[:, :half] + flip(x[:, half:], "fsdp", 1, n)
    half = half // 2
    return x[:, :half] + flip(x[:, half:], "fsdp", 2, n)


def sum_fsdp(x, n):
    if n != 4:
        return lax.psum(x, "fsdp")
    x = x + flip(x, "fsdp", 1, n)
    return x + flip(x, "fsdp", 2, n)


def reorder(x, member, n):
    if n != 4:
        return x
    width = x.shape[1] // n
    return jnp.concatenate(
        [lax.dynamic_slice_in_dim(x, (member ^ k) * width, width, 1) for k in (0, 2, 1, 3)], axis=1
    )


def restore(x, member, n):
    if n != 4:
        return x
    width = x.shape[1] // n
    places = []
    for k in range(n):
        wanted = member ^ k
        places.append((wanted & 1) * 2 + (wanted >> 1))
    return jnp.concatenate(
        [lax.dynamic_slice_in_dim(x, place * width, width, 1) for place in places], axis=1
    )


def gather_tokens(x, swap):
    near = jnp.concatenate([x, flip(x, "ctx", 1, 4)], axis=0)
    far = jnp.concatenate([flip(x, "ctx", 2, 4), flip(x, "ctx", 3, 4)], axis=0)
    return jnp.concatenate([jnp.where(swap, far, near), jnp.where(swap, near, far)], axis=0)


def reduce_tokens(x):
    rows = x.shape[0] // 4
    cols = x.shape[1] // 2
    left, right = x[:, :cols], x[:, cols:]
    from_tp = tp_swap(left[2 * rows :].astype(BF))
    odd = jnp.concatenate([right[rows : 2 * rows], right[3 * rows :]], axis=0)
    even = jnp.concatenate([right[:rows], right[2 * rows : 3 * rows]], axis=0)
    from_pair = pair_swap(odd.astype(BF))
    left = left[: 2 * rows] + from_tp.astype(F32)
    right = even + from_pair.astype(F32)
    last_left = pair_swap(left[rows:].astype(BF))
    last_right = tp_swap(right[rows:].astype(BF))
    return jnp.concatenate(
        [left[:rows] + last_left.astype(F32), right[:rows] + last_right.astype(F32)], axis=1
    )


def spread_tokens(x):
    rows = x.shape[0]
    cols = x.shape[1] // 2
    left, right = x[:, :cols], x[:, cols:]
    left = jnp.concatenate([left, pair_swap(left)], axis=0)
    right_tp = tp_swap(right)
    left_far = tp_swap(left)
    right_far = pair_swap(jnp.concatenate([right, right_tp], axis=0))
    left = jnp.concatenate([left, left_far], axis=0)
    right = jnp.concatenate([right, right_far[:rows], right_tp, right_far[rows:]], axis=0)
    return jnp.concatenate([left, right], axis=1)


def unit_norm(x):
    center = x - jnp.mean(x, axis=-1, keepdims=True)
    inverse = lax.rsqrt(jnp.mean(center * center, axis=-1, keepdims=True) + EPSILON)
    return center * inverse, inverse


def rotary_tables(positions, heads):
    half = ROT // 2
    frequency = jnp.exp(jnp.arange(half).astype(F32) * (-2.0 * math.log(10000.0) / ROT))
    angles = positions[:, None] * frequency[None, :]
    cosine, sine = jnp.cos(angles), jnp.sin(angles)
    rows = positions.shape[0]
    ones = jnp.ones((rows, HD - ROT), F32)
    zeros = jnp.zeros((rows, HD - ROT), F32)
    none = jnp.zeros((rows, half), F32)
    scale = jnp.concatenate([cosine, cosine, ones], axis=1)
    ahead = jnp.concatenate([-sine, none, zeros], axis=1)
    behind = jnp.concatenate([none, sine, zeros], axis=1)
    return tuple(jnp.tile(table, (1, heads)) for table in (scale, ahead, behind))


def rotate(x, tables, sign):
    half = ROT // 2
    scale, ahead, behind = tables
    return x * scale + sign * (
        jnp.roll(x, -half, axis=1) * ahead + jnp.roll(x, half, axis=1) * behind
    )


def gelu_pair(inputs):
    normal_cdf = 0.5 * (1.0 + lax.erf(inputs * (1.0 / math.sqrt(2.0))))
    density = jnp.exp(-0.5 * inputs * inputs) * (1.0 / math.sqrt(2.0 * math.pi))
    return (inputs * normal_cdf, normal_cdf + inputs * density)


def heads_of(x):
    return x.reshape(x.shape[0], x.shape[1] // HD, HD)


def layer_forward(unit, weights, allowed, tables):
    up, qkv, down_t, dense_t, vectors = weights
    attn_gain, attn_shift, mlp_gain, mlp_shift, up_bias, qkv_bias = vectors
    width = qkv.shape[1] // 3
    unit = unit.astype(F32)
    attn_in = (unit * attn_gain + attn_shift).astype(BF)
    mlp_in = (unit * mlp_gain + mlp_shift).astype(BF)
    raw = dot(attn_in, qkv, ((1,), (0,))) + qkv_bias
    queries = rotate(raw[:, :width], tables, 1.0).astype(BF)
    keys = rotate(raw[:, width : 2 * width], tables, 1.0).astype(BF)
    values = raw[:, 2 * width :].astype(BF)
    scores = jnp.einsum(
        "qhd,khd->hqk", heads_of(queries), heads_of(keys), preferred_element_type=F32
    ) * (1.0 / math.sqrt(HD))
    scores = jnp.where(allowed[None], scores, MASKED)
    weighted = jnp.exp(scores - jnp.max(scores, axis=-1, keepdims=True))
    probs = weighted / jnp.sum(weighted, axis=-1, keepdims=True)
    attended = jnp.einsum(
        "hqk,khd->qhd", probs.astype(BF), heads_of(values), preferred_element_type=F32
    )
    attended = attended.astype(BF).reshape(unit.shape[0], width)
    pre = dot(mlp_in, up, ((1,), (0,))) + up_bias
    activated, slopes = gelu_pair(pre)
    activated = activated.astype(BF)
    partial = dot(activated, down_t, ((1,), (1,))) + dot(attended, dense_t, ((1,), (1,)))
    return partial, (attn_in, mlp_in, queries, keys, values, probs, attended, activated, slopes)


def layer_backward(upstream, unit, weights, stored, tables):
    up, qkv, down_t, dense_t, vectors = weights
    attn_gain, attn_shift, mlp_gain, mlp_shift, up_bias, qkv_bias = vectors
    attn_in, mlp_in, queries, keys, values, probs, attended, activated, slopes = stored
    width = qkv.shape[1] // 3
    rows = upstream.shape[0]
    unit = unit.astype(F32)
    grad_down = dot(upstream, activated, ((0,), (0,)))
    grad_dense = dot(upstream, attended, ((0,), (0,)))
    grad_pre = dot(upstream, down_t, ((1,), (0,))) * slopes
    grad_pre_low = grad_pre.astype(BF)
    grad_up = dot(mlp_in, grad_pre_low, ((0,), (0,)))
    into_mlp = dot(grad_pre_low, up, ((1,), (1,)))
    grad_att = dot(upstream, dense_t, ((1,), (0,))).astype(BF)
    grad_heads = heads_of(grad_att)
    delta = jnp.einsum(
        "qhd,qhd->hq", grad_heads, heads_of(attended), preferred_element_type=F32
    )
    grad_prob = jnp.einsum("qhd,khd->hqk", grad_heads, heads_of(values), preferred_element_type=F32)
    grad_score = (probs * (grad_prob - delta[:, :, None])).astype(BF)
    inv_root = 1.0 / math.sqrt(HD)
    grad_query = (
        jnp.einsum("hqk,khd->qhd", grad_score, heads_of(keys), preferred_element_type=F32)
        .reshape(rows, width)
    )
    grad_key = (
        jnp.einsum("hqk,qhd->khd", grad_score, heads_of(queries), preferred_element_type=F32)
        .reshape(rows, width)
    )
    grad_value = jnp.einsum(
        "hqk,qhd->khd", probs.astype(BF), grad_heads, preferred_element_type=F32
    ).reshape(rows, width)
    pieces = jnp.concatenate(
        [
            rotate(grad_query * inv_root, tables, -1.0),
            rotate(grad_key * inv_root, tables, -1.0),
            grad_value,
        ],
        axis=1,
    )
    pieces_low = pieces.astype(BF)
    grad_qkv = dot(attn_in, pieces_low, ((0,), (0,)))
    into_attn = dot(pieces_low, qkv, ((1,), (1,)))
    mixed = into_attn * attn_gain + into_mlp * mlp_gain
    sums = jnp.stack(
        [
            jnp.sum(into_attn * unit, axis=0),
            jnp.sum(into_attn, axis=0),
            jnp.sum(into_mlp * unit, axis=0),
            jnp.sum(into_mlp, axis=0),
        ]
    )
    slice_sums = jnp.concatenate([jnp.sum(grad_pre, axis=0), jnp.sum(pieces, axis=0)])
    return mixed, (grad_down, grad_dense, grad_up, grad_qkv), sums, slice_sums


def make_body(n):
    def on_device(
        hidden_in,
        cotangent,
        segments,
        attn_gain,
        attn_shift,
        qkv_weight,
        qkv_bias,
        dense_weight,
        dense_bias,
        mlp_gain,
        mlp_shift,
        up_weight,
        up_bias,
        down_weight,
        down_bias,
    ):
        member = lax.axis_index("fsdp")
        place = lax.axis_index("ctx")
        side = lax.axis_index("tp")
        bit = place & 1
        pair = place >> 1
        rows = hidden_in.shape[1]
        units = up_weight.shape[2] // 2
        width = qkv_weight.shape[3] // 2
        features = hidden_in.shape[2]

        start_hidden = gather_tokens(reorder(hidden_in[0], member, n), pair != side)

        shard = attn_gain.shape[1]
        small = jnp.concatenate(
            [
                vector.reshape(LAYERS, -1)
                for vector in (
                    attn_gain,
                    attn_shift,
                    mlp_gain,
                    mlp_shift,
                    dense_bias,
                    down_bias,
                    up_bias,
                    qkv_bias,
                )
            ],
            axis=1,
        )[None]
        small = gather_rows(small, n).astype(F32)
        half_members = n // 2
        own_rows = bit * half_members + jnp.arange(half_members)
        if n == 4:
            wanted = member ^ own_rows
            own_rows = (wanted & 1) * 2 + (wanted >> 1)
        chosen = small[own_rows]
        up_chunk = up_bias.shape[1]
        qkv_chunk = qkv_bias.shape[2]

        def small_of(layer):
            feature_vectors = [
                small[:, layer, k * shard : (k + 1) * shard].reshape(1, features) for k in range(6)
            ]
            first = 6 * shard
            up_part = chosen[:, layer, first : first + up_chunk].reshape(1, units)
            first = first + up_chunk
            qkv_part = chosen[:, layer, first:].reshape(half_members, 3, qkv_chunk)
            qkv_part = jnp.swapaxes(qkv_part, 0, 1).reshape(1, 3 * width)
            return feature_vectors, up_part, qkv_part

        def weights_of(layer):
            up = lax.dynamic_slice_in_dim(up_weight[layer], bit * units, units, 1)
            qkv = lax.dynamic_slice_in_dim(qkv_weight[layer], bit * width, width, 2)
            qkv = jnp.concatenate([qkv[0], qkv[1], qkv[2]], axis=1)
            down_t = lax.dynamic_slice_in_dim(down_weight[layer], bit * units, units, 0).T
            dense_t = lax.dynamic_slice_in_dim(dense_weight[layer], bit * width, width, 0).T
            vectors, up_part, qkv_part = small_of(layer)
            return (
                gather_rows(up, n),
                gather_rows(qkv, n),
                gather_rows(down_t, n),
                gather_rows(dense_t, n),
                (vectors[0], vectors[1], vectors[2], vectors[3], up_part, qkv_part),
            ), vectors[4] + vectors[5]

        quarters = (2 * side + bit) ^ jnp.arange(4, dtype=jnp.int32)
        positions = (quarters[:, None] * rows + jnp.arange(rows, dtype=jnp.int32)).reshape(-1)
        seg_row = segments[0].reshape(4, rows)[quarters].reshape(-1)
        allowed = (seg_row[:, None] == seg_row[None, :]) & (
            positions[None, :] <= positions[:, None]
        )
        tables = rotary_tables(positions.astype(F32), width // HD)

        held = [weights_of(layer) for layer in range(LAYERS)]
        upstream_low = gather_tokens(reorder(cotangent[0], member, n), pair != side)

        hidden = start_hidden[:rows].astype(F32)
        unit_all, inverse_all = unit_norm(start_hidden.astype(F32))
        own_unit, own_inverse = unit_all[:rows], inverse_all[:rows]
        unit_low = unit_all.astype(BF)
        kept = []
        for layer in range(LAYERS):
            weights, out_bias = held[layer]
            partial, stored = layer_forward(unit_low, weights, allowed, tables)
            kept.append((unit_low, own_unit, own_inverse, stored))
            hidden = hidden + reduce_tokens(partial) + out_bias
            if layer + 1 < LAYERS:
                own_unit, own_inverse = unit_norm(hidden)
                unit_low = spread_tokens(own_unit.astype(BF))

        owner = side == pair

        def share(x):
            moves = [(c * 2 + (c >> 1), c * 2 + 1 - (c >> 1)) for c in range(4)]
            other = lax.ppermute(x, ("ctx", "tp"), moves)
            return restore(jnp.where(owner, x, other), member, n)

        hidden_out = share(hidden.astype(BF))

        upstream = upstream_low[:rows].astype(F32)
        results = [None] * LAYERS
        for layer in reversed(range(LAYERS)):
            weights, _ = held[layer]
            unit_low, own_unit, own_inverse, stored = kept[layer]
            mixed, grads, sums, slice_sums = layer_backward(
                upstream_low, unit_low, weights, stored, tables
            )
            bias_sum = jnp.sum(upstream, axis=0, keepdims=True)
            reduced = reduce_tokens(mixed)
            upstream = upstream + own_inverse * (
                reduced
                - jnp.mean(reduced, axis=-1, keepdims=True)
                - own_unit * jnp.mean(reduced * own_unit, axis=-1, keepdims=True)
            )
            if layer > 0:
                upstream_low = spread_tokens(upstream.astype(BF))
            big = []
            for grad in grads:
                own = scatter_rows(grad, n).astype(BF)
                big.append((own, pair_swap(own)))
            sums = jnp.concatenate([sums, bias_sum], axis=0)
            sums = sums + tp_swap(sums)
            sums = sums + pair_swap(sums)
            sums = scatter_columns(sums, n)
            slice_sums = sum_fsdp(slice_sums[None], n)
            slice_sums = (slice_sums, pair_swap(slice_sums))
            results[layer] = (big, sums, slice_sums)

        grad_input = share(upstream.astype(BF)).astype(F32)

        def ordered(two):
            own, other = two
            return jnp.where(bit == 0, own, other), jnp.where(bit == 0, other, own)

        outputs = [[] for _ in range(12)]
        for layer in range(LAYERS):
            big, sums, slice_sums = results[layer]
            down, dense, up, qkv = [ordered(two) for two in big]
            outputs[0].append(sums[0])
            outputs[1].append(sums[1])
            outputs[2].append(
                jnp.concatenate(
                    [jnp.swapaxes(part.reshape(-1, 3, width), 0, 1) for part in qkv], axis=2
                ).astype(F32)
            )
            first, second = ordered(slice_sums)
            both = jnp.stack([first[0], second[0]])
            qkv_sums = jnp.swapaxes(both[:, units:].reshape(2, 3, width), 0, 1).reshape(3, -1)
            outputs[3].append(
                lax.dynamic_slice_in_dim(qkv_sums, member * qkv_chunk, qkv_chunk, 1)
            )
            outputs[4].append(jnp.concatenate([part.T for part in dense], axis=0).astype(F32))
            outputs[5].append(sums[4])
            outputs[6].append(sums[2])
            outputs[7].append(sums[3])
            outputs[8].append(jnp.concatenate(up, axis=1).astype(F32))
            outputs[9].append(
                lax.dynamic_slice_in_dim(
                    both[:, :units].reshape(-1), member * up_chunk, up_chunk, 0
                )
            )
            outputs[10].append(jnp.concatenate([part.T for part in down], axis=0).astype(F32))
            outputs[11].append(sums[4])
        return (hidden_out[None], grad_input[None]) + tuple(jnp.stack(out) for out in outputs)

    return on_device


def solution(mesh):
    return jax.shard_map(
        make_body(mesh.shape["fsdp"]),
        mesh=mesh,
        in_specs=(
            P("fsdp", "ctx", None),
            P("fsdp", "ctx", None),
            P("fsdp", None),
            P(None, "fsdp"),
            P(None, "fsdp"),
            P(None, None, "fsdp", "tp"),
            P(None, None, ("tp", "fsdp")),
            P(None, "tp", "fsdp"),
            P(None, "fsdp"),
            P(None, "fsdp"),
            P(None, "fsdp"),
            P(None, "fsdp", "tp"),
            P(None, ("tp", "fsdp")),
            P(None, "tp", "fsdp"),
            P(None, "fsdp"),
        ),
        out_specs=(
            P("fsdp", "ctx", None),
            P("fsdp", "ctx", None),
            P(None, "fsdp"),
            P(None, "fsdp"),
            P(None, None, "fsdp", "tp"),
            P(None, None, ("tp", "fsdp")),
            P(None, "tp", "fsdp"),
            P(None, "fsdp"),
            P(None, "fsdp"),
            P(None, "fsdp"),
            P(None, "fsdp", "tp"),
            P(None, ("tp", "fsdp")),
            P(None, "tp", "fsdp"),
            P(None, "fsdp"),
        ),
        check_vma=False,
    )
```

```python
import math

import jax
import jax.numpy as jnp
from jax import lax
from jax.experimental import pallas as pl
from jax.experimental.pallas import tpu as pltpu
from jax.sharding import PartitionSpec as P

HD = 64
ROT = 16
LAYERS = 2
EPSILON = 1e-05
MASKED = -1e30
BF = jnp.bfloat16
F32 = jnp.float32


def flip(x, axis, bits, count):
    return lax.ppermute(x, axis, [(i, i ^ bits) for i in range(count)])


def tp_swap(x):
    return flip(x, "tp", 1, 2)


def pair_swap(x):
    return flip(x, "ctx", 1, 4)


def dot(a, b, dims):
    return lax.dot_general(a, b, (dims, ((), ())), preferred_element_type=F32)


def gather_rows(x, n):
    if n != 4:
        return lax.all_gather(x, "fsdp", axis=0, tiled=True)
    near, far = gather_halves(x, n)
    return jnp.concatenate([near, far], axis=0)


def gather_halves(x, n):
    if n != 4:
        whole = lax.all_gather(x, "fsdp", axis=0, tiled=True)
        half = whole.shape[0] // 2
        return whole[:half], whole[half:]
    both = jnp.concatenate([x, flip(x, "fsdp", 2, n)], axis=0)
    return both, flip(both, "fsdp", 1, n)


def scatter_rows(keep, send, n):
    if n != 4:
        whole = jnp.concatenate([keep, send.astype(F32)], axis=0)
        return lax.psum_scatter(whole, "fsdp", scatter_dimension=0, tiled=True)
    x = keep + flip(send, "fsdp", 1, n).astype(F32)
    half = x.shape[0] // 2
    return x[:half] + flip(x[half:].astype(BF), "fsdp", 2, n).astype(F32)


def scatter_columns(x, n):
    if n != 4:
        return lax.psum_scatter(x, "fsdp", scatter_dimension=1, tiled=True)
    half = x.shape[1] // 2
    x = x[:, :half] + flip(x[:, half:], "fsdp", 1, n)
    half = half // 2
    return x[:, :half] + flip(x[:, half:], "fsdp", 2, n)


def sum_fsdp(x, n):
    if n != 4:
        return lax.psum(x, "fsdp")
    x = x + flip(x, "fsdp", 1, n)
    return x + flip(x, "fsdp", 2, n)


def reorder(x, member, n):
    if n != 4:
        return x
    width = x.shape[1] // n
    return jnp.concatenate(
        [lax.dynamic_slice_in_dim(x, (member ^ k) * width, width, 1) for k in (0, 2, 1, 3)], axis=1
    )


def restore(x, member, n):
    if n != 4:
        return x
    width = x.shape[1] // n
    places = []
    for k in range(n):
        wanted = member ^ k
        places.append((wanted & 1) * 2 + (wanted >> 1))
    return jnp.concatenate(
        [lax.dynamic_slice_in_dim(x, place * width, width, 1) for place in places], axis=1
    )


def gather_tokens(x, swap):
    near = jnp.concatenate([x, flip(x, "ctx", 1, 4)], axis=0)
    far = jnp.concatenate([flip(x, "ctx", 2, 4), flip(x, "ctx", 3, 4)], axis=0)
    return jnp.concatenate([jnp.where(swap, far, near), jnp.where(swap, near, far)], axis=0)


def reduce_tokens(near_left, far_left, even_right, odd_right):
    rows = near_left.shape[0] // 2
    left = near_left + tp_swap(far_left).astype(F32)
    right = even_right + pair_swap(odd_right).astype(F32)
    last_left = pair_swap(left[rows:].astype(BF))
    last_right = tp_swap(right[rows:].astype(BF))
    return jnp.concatenate(
        [left[:rows] + last_left.astype(F32), right[:rows] + last_right.astype(F32)], axis=1
    )


def spread_tokens(x):
    rows = x.shape[0]
    cols = x.shape[1] // 2
    left, right = x[:, :cols], x[:, cols:]
    left = jnp.concatenate([left, pair_swap(left)], axis=0)
    right_tp = tp_swap(right)
    left_far = tp_swap(left)
    right_far = pair_swap(jnp.concatenate([right, right_tp], axis=0))
    left = jnp.concatenate([left, left_far], axis=0)
    right = jnp.concatenate([right, right_far[:rows], right_tp, right_far[rows:]], axis=0)
    return jnp.concatenate([left, right], axis=1)


def unit_norm(x):
    center = x - jnp.mean(x, axis=-1, keepdims=True)
    inverse = lax.rsqrt(jnp.mean(center * center, axis=-1, keepdims=True) + EPSILON)
    return center * inverse, inverse


def rotary_tables(positions, heads):
    half = ROT // 2
    frequency = jnp.exp(jnp.arange(half).astype(F32) * (-2.0 * math.log(10000.0) / ROT))
    angles = positions[:, None] * frequency[None, :]
    cosine, sine = jnp.cos(angles), jnp.sin(angles)
    rows = positions.shape[0]
    ones = jnp.ones((rows, HD - ROT), F32)
    zeros = jnp.zeros((rows, HD - ROT), F32)
    scale = jnp.concatenate([cosine, cosine, ones], axis=1)
    cross = jnp.concatenate([sine, sine, zeros], axis=1)
    source = jnp.arange(heads * HD)[:, None]
    target = jnp.arange(heads * HD)[None, :]
    spot = target % HD
    turn = jnp.where((spot < half) & (source == target + half), -1.0, 0.0)
    turn = jnp.where((spot >= half) & (spot < ROT) & (source == target - half), 1.0, turn)
    return jnp.tile(scale, (1, heads)), jnp.tile(cross, (1, heads)), turn.astype(BF)


def turned(x, turn):
    high = x.astype(BF)
    low = (x - high.astype(F32)).astype(BF)
    return nn(high, turn) + nn(low, turn)


def nn(a, b):
    return dot(a, b, ((1,), (0,)))


def nt(a, b):
    return dot(a, b, ((1,), (1,)))


def tn(a, b):
    return dot(a, b, ((0,), (0,)))


def gelu_pair(inputs):
    normal_cdf = 0.5 * (1.0 + lax.erf(inputs * (1.0 / math.sqrt(2.0))))
    density = jnp.exp(-0.5 * inputs * inputs) * (1.0 / math.sqrt(2.0 * math.pi))
    return (inputs * normal_cdf, normal_cdf + inputs * density)


BLOCK = 128


def forward_kernel(
    unit, wa, wb, vectors, up_bias, qkv_bias, scale, cross, turn, mask,
    near_left, far_left, even_right, odd_right, slopes, act, att, queries, keys, values, probs,
):
    total, features = unit.shape
    half = features // 2
    units = act.shape[1]
    width = att.shape[1]
    first = 2 * units
    last = first + 3 * width

    def project(i, carry):
        rows = pl.ds(pl.multiple_of(i * BLOCK, BLOCK), BLOCK)
        x = unit[rows, :].astype(F32)
        attn_in = (x * vectors[0:1, :] + vectors[1:2, :]).astype(BF)
        mlp_in = (x * vectors[2:3, :] + vectors[3:4, :]).astype(BF)
        raw = nn(attn_in[:, :half], wa[:, first:last]) + nn(attn_in[:, half:], wb[:, first:last])
        raw = raw + qkv_bias[...]
        q, k, v = raw[:, :width], raw[:, width : 2 * width], raw[:, 2 * width :]
        queries[rows, :] = (q * scale[rows, :] + turned(q, turn[...]) * cross[rows, :]).astype(BF)
        keys[rows, :] = (k * scale[rows, :] + turned(k, turn[...]) * cross[rows, :]).astype(BF)
        values[rows, :] = v.astype(BF)
        pre = nn(mlp_in[:, :half], wa[:, :units]) + nn(mlp_in[:, half:], wb[:, :units])
        activated, slope = gelu_pair(pre + up_bias[...])
        act[rows, :] = activated.astype(BF)
        slopes[rows, :] = slope
        return carry

    lax.fori_loop(0, total // BLOCK, project, 0)

    def attend(i, carry):
        rows = pl.ds(pl.multiple_of(i * BLOCK, BLOCK), BLOCK)
        for head in range(width // HD):
            cols = slice(head * HD, (head + 1) * HD)
            scores = nt(queries[rows, cols], keys[:, cols]) * (1.0 / math.sqrt(HD)) + mask[rows, :]
            weighted = jnp.exp(scores - jnp.max(scores, axis=1, keepdims=True))
            chance = (weighted * (1.0 / jnp.sum(weighted, axis=1, keepdims=True))).astype(BF)
            probs[head, rows, :] = chance
            att[rows, cols] = nn(chance, values[:, cols]).astype(BF)
        return carry

    lax.fori_loop(0, total // BLOCK, attend, 0)

    quarter = total // 4
    for i in range(4):
        rows = slice(i * quarter, (i + 1) * quarter)
        left = nt(act[rows, :], wa[:, units:first]) + nt(att[rows, :], wa[:, last:])
        right = nt(act[rows, :], wb[:, units:first]) + nt(att[rows, :], wb[:, last:])
        place_quarter(i, quarter, left, right, near_left, far_left, even_right, odd_right)


def place_quarter(i, quarter, left, right, near_left, far_left, even_right, odd_right):
    low = slice((i % 2) * quarter, (i % 2 + 1) * quarter)
    high = slice((i // 2) * quarter, (i // 2 + 1) * quarter)
    if i < 2:
        near_left[low, :] = left
    else:
        far_left[low, :] = left.astype(BF)
    if i % 2 == 0:
        even_right[high, :] = right
    else:
        odd_right[high, :] = right.astype(BF)


def mlp_back_kernel(
    upstream, unit, wa, wb, vectors, act, att, slopes,
    keep, send, mixed, grad_att, sums,
    grad_low, mlp_in,
):
    total, features = unit.shape
    half = features // 2
    units = act.shape[1]
    first = 2 * units
    last = wa.shape[1] - att.shape[1]
    sums[...] = jnp.zeros_like(sums)

    def rows_back(i, carry):
        rows = pl.ds(pl.multiple_of(i * BLOCK, BLOCK), BLOCK)
        up = upstream[rows, :]
        x = unit[rows, :].astype(F32)
        mlp_in[rows, :] = (x * vectors[2:3, :] + vectors[3:4, :]).astype(BF)
        grad = nn(up[:, :half], wa[:, units:first]) + nn(up[:, half:], wb[:, units:first])
        grad = grad * slopes[rows, :]
        low = grad.astype(BF)
        grad_low[rows, :] = low
        sums[2:3, :] = sums[2:3, :] + jnp.sum(grad, axis=0, keepdims=True)
        grad_att[rows, :] = (nn(up[:, :half], wa[:, last:]) + nn(up[:, half:], wb[:, last:])).astype(BF)
        for part, w in ((slice(0, half), wa), (slice(half, features), wb)):
            into = nt(low, w[:, :units])
            mixed[rows, part] = into * vectors[2:3, part]
            sums[0:1, part] = sums[0:1, part] + jnp.sum(into * x[:, part], axis=0, keepdims=True)
            sums[1:2, part] = sums[1:2, part] + jnp.sum(into, axis=0, keepdims=True)
        return carry

    lax.fori_loop(0, total // BLOCK, rows_back, 0)

    for start in range(0, half, BLOCK):
        rows = slice(start, start + BLOCK)
        far = slice(half + start, half + start + BLOCK)
        keep[rows, :units] = tn(mlp_in[:, rows], grad_low[...])
        send[rows, :units] = tn(mlp_in[:, far], grad_low[...]).astype(BF)
        keep[rows, units:first] = tn(upstream[:, rows], act[...])
        send[rows, units:first] = tn(upstream[:, far], act[...]).astype(BF)
        keep[rows, first:] = tn(upstream[:, rows], att[...])
        send[rows, first:] = tn(upstream[:, far], att[...]).astype(BF)


def attention_back_kernel(
    unit, wa, wb, vectors, scale, cross, turn, queries, keys, values, probs, att, grad_att, mixed,
    keep, send, near_left, far_left, even_right, odd_right, sums, slice_sums,
    dq, dk, dv, pieces, attn_in,
):
    total, features = unit.shape
    half = features // 2
    width = att.shape[1]
    last = wa.shape[1] - width
    first = last - 3 * width
    dk[...] = jnp.zeros_like(dk)
    dv[...] = jnp.zeros_like(dv)
    sums[...] = jnp.zeros_like(sums)
    slice_sums[...] = jnp.zeros_like(slice_sums)

    def attend(i, carry):
        rows = pl.ds(pl.multiple_of(i * BLOCK, BLOCK), BLOCK)
        x = unit[rows, :].astype(F32)
        attn_in[rows, :] = (x * vectors[0:1, :] + vectors[1:2, :]).astype(BF)
        for head in range(width // HD):
            cols = slice(head * HD, (head + 1) * HD)
            grad = grad_att[rows, cols]
            delta = jnp.sum(grad.astype(F32) * att[rows, cols].astype(F32), axis=1, keepdims=True)
            chance = probs[head, rows, :]
            change = chance.astype(F32) * (nt(grad, values[:, cols]) - delta)
            change = (change * (1.0 / math.sqrt(HD))).astype(BF)
            dq[rows, cols] = nn(change, keys[:, cols])
            dk[:, cols] = dk[:, cols] + tn(change, queries[rows, cols])
            dv[:, cols] = dv[:, cols] + tn(chance, grad)
        return carry

    lax.fori_loop(0, total // BLOCK, attend, 0)

    quarter = total // 4
    for i in range(4):
        rows = slice(i * quarter, (i + 1) * quarter)
        q, k, v = dq[rows, :], dk[rows, :], dv[rows, :]
        q = q * scale[rows, :] - turned(q, turn[...]) * cross[rows, :]
        k = k * scale[rows, :] - turned(k, turn[...]) * cross[rows, :]
        for number, piece in enumerate((q, k, v)):
            spot = slice(number * width, (number + 1) * width)
            pieces[rows, spot] = piece.astype(BF)
            slice_sums[0:1, spot] = slice_sums[0:1, spot] + jnp.sum(piece, axis=0, keepdims=True)
        low = pieces[rows, :]
        x = unit[rows, :].astype(F32)
        halves = []
        for part, w in ((slice(0, half), wa), (slice(half, features), wb)):
            into = nt(low, w[:, first:last])
            sums[0:1, part] = sums[0:1, part] + jnp.sum(into * x[:, part], axis=0, keepdims=True)
            sums[1:2, part] = sums[1:2, part] + jnp.sum(into, axis=0, keepdims=True)
            halves.append(into * vectors[0:1, part] + mixed[rows, part])
        place_quarter(i, quarter, halves[0], halves[1], near_left, far_left, even_right, odd_right)

    for start in range(0, half, BLOCK):
        rows = slice(start, start + BLOCK)
        far = slice(half + start, half + start + BLOCK)
        keep[rows, :] = tn(attn_in[:, rows], pieces[...])
        send[rows, :] = tn(attn_in[:, far], pieces[...]).astype(BF)


def call(kernel, outs, args, scratch=()):
    return pl.pallas_call(
        kernel,
        out_shape=tuple(jax.ShapeDtypeStruct(shape, dtype) for shape, dtype in outs),
        in_specs=[pl.BlockSpec(memory_space=pltpu.VMEM)] * len(args),
        out_specs=[pl.BlockSpec(memory_space=pltpu.VMEM)] * len(outs),
        scratch_shapes=[pltpu.VMEM(shape, dtype) for shape, dtype in scratch],
        compiler_params=pltpu.CompilerParams(vmem_limit_bytes=48 * 1024 * 1024),
    )(*args)


def split_outs(rows, features):
    shape = (rows // 2, features // 2)
    return [(shape, F32), (shape, BF), (shape, F32), (shape, BF)]


def layer_forward(unit, weights, mask, tables):
    wa, wb, vectors, up_bias, qkv_bias = weights
    rows, features = unit.shape
    units, width = up_bias.shape[1], qkv_bias.shape[1] // 3
    heads = width // HD
    outs = call(
        forward_kernel,
        split_outs(rows, features)
        + [((rows, units), F32), ((rows, units), BF)]
        + [((rows, width), BF)] * 4
        + [((heads, rows, rows), BF)],
        (unit, wa, wb, vectors, up_bias, qkv_bias) + tables + (mask,),
    )
    return outs[:4], outs[4:]


def layer_backward(upstream, unit, weights, stored, tables):
    wa, wb, vectors, up_bias, qkv_bias = weights
    slopes, act, att, queries, keys, values, probs = stored
    rows, features = unit.shape
    half = features // 2
    units, width = up_bias.shape[1], qkv_bias.shape[1] // 3
    wide = 2 * units + width
    keep, send, mixed, grad_att, mlp_sums = call(
        mlp_back_kernel,
        [
            ((half, wide), F32),
            ((half, wide), BF),
            ((rows, features), F32),
            ((rows, width), BF),
            ((8, features), F32),
        ],
        (upstream, unit, wa, wb, vectors, act, att, slopes),
        [((rows, units), BF), ((rows, features), BF)],
    )
    outs = call(
        attention_back_kernel,
        [((half, 3 * width), F32), ((half, 3 * width), BF)]
        + split_outs(rows, features)
        + [((8, features), F32), ((8, 3 * width), F32)],
        (unit, wa, wb, vectors)
        + tables
        + (queries, keys, values, probs, att, grad_att, mixed),
        [((rows, width), F32)] * 3 + [((rows, 3 * width), BF), ((rows, features), BF)],
    )
    sums = jnp.concatenate([outs[6][:2], mlp_sums[:2]], axis=0)
    slice_sums = jnp.concatenate([mlp_sums[2], outs[7][0]])
    return outs[2:6], ((keep, send), (outs[0], outs[1])), sums, slice_sums


def make_body(n):
    def on_device(
        hidden_in,
        cotangent,
        segments,
        attn_gain,
        attn_shift,
        qkv_weight,
        qkv_bias,
        dense_weight,
        dense_bias,
        mlp_gain,
        mlp_shift,
        up_weight,
        up_bias,
        down_weight,
        down_bias,
    ):
        member = lax.axis_index("fsdp")
        place = lax.axis_index("ctx")
        side = lax.axis_index("tp")
        bit = place & 1
        pair = place >> 1
        rows = hidden_in.shape[1]
        units = up_weight.shape[2] // 2
        width = qkv_weight.shape[3] // 2
        features = hidden_in.shape[2]

        start_hidden = gather_tokens(reorder(hidden_in[0], member, n), pair != side)

        shard = attn_gain.shape[1]
        small = jnp.concatenate(
            [
                vector.reshape(LAYERS, -1)
                for vector in (
                    attn_gain,
                    attn_shift,
                    mlp_gain,
                    mlp_shift,
                    dense_bias,
                    down_bias,
                    up_bias,
                    qkv_bias,
                )
            ],
            axis=1,
        )[None]
        small = gather_rows(small, n).astype(F32)
        half_members = n // 2
        own_rows = bit * half_members + jnp.arange(half_members)
        if n == 4:
            wanted = member ^ own_rows
            own_rows = (wanted & 1) * 2 + (wanted >> 1)
        chosen = small[own_rows]
        up_chunk = up_bias.shape[1]
        qkv_chunk = qkv_bias.shape[2]

        def small_of(layer):
            feature_vectors = [
                small[:, layer, k * shard : (k + 1) * shard].reshape(1, features) for k in range(6)
            ]
            first = 6 * shard
            up_part = chosen[:, layer, first : first + up_chunk].reshape(1, units)
            first = first + up_chunk
            qkv_part = chosen[:, layer, first:].reshape(half_members, 3, qkv_chunk)
            qkv_part = jnp.swapaxes(qkv_part, 0, 1).reshape(1, 3 * width)
            return feature_vectors, up_part, qkv_part

        def weights_of(layer):
            up = lax.dynamic_slice_in_dim(up_weight[layer], bit * units, units, 1)
            qkv = lax.dynamic_slice_in_dim(qkv_weight[layer], bit * width, width, 2)
            down_t = lax.dynamic_slice_in_dim(down_weight[layer], bit * units, units, 0).T
            dense_t = lax.dynamic_slice_in_dim(dense_weight[layer], bit * width, width, 0).T
            packed = jnp.concatenate([up, down_t, qkv[0], qkv[1], qkv[2], dense_t], axis=1)
            wa, wb = gather_halves(packed, n)
            vectors, up_part, qkv_part = small_of(layer)
            rows4 = jnp.concatenate(vectors[:4], axis=0)
            return (wa, wb, rows4, up_part, qkv_part), vectors[4] + vectors[5]

        quarters = (2 * side + bit) ^ jnp.arange(4, dtype=jnp.int32)
        positions = (quarters[:, None] * rows + jnp.arange(rows, dtype=jnp.int32)).reshape(-1)
        seg_row = segments[0].reshape(4, rows)[quarters].reshape(-1)
        allowed = (seg_row[:, None] == seg_row[None, :]) & (
            positions[None, :] <= positions[:, None]
        )
        mask = jnp.where(allowed, 0.0, MASKED).astype(F32)
        tables = rotary_tables(positions.astype(F32), width // HD)

        held = [weights_of(layer) for layer in range(LAYERS)]
        upstream_low = gather_tokens(reorder(cotangent[0], member, n), pair != side)

        hidden = start_hidden[:rows].astype(F32)
        unit_all, inverse_all = unit_norm(start_hidden.astype(F32))
        own_unit, own_inverse = unit_all[:rows], inverse_all[:rows]
        unit_low = unit_all.astype(BF)
        kept = []
        for layer in range(LAYERS):
            weights, out_bias = held[layer]
            partial, stored = layer_forward(unit_low, weights, mask, tables)
            kept.append((unit_low, own_unit, own_inverse, stored))
            hidden = hidden + reduce_tokens(*partial) + out_bias
            if layer + 1 < LAYERS:
                own_unit, own_inverse = unit_norm(hidden)
                unit_low = spread_tokens(own_unit.astype(BF))

        owner = side == pair

        def share(x):
            moves = [(c * 2 + (c >> 1), c * 2 + 1 - (c >> 1)) for c in range(4)]
            other = lax.ppermute(x, ("ctx", "tp"), moves)
            return restore(jnp.where(owner, x, other), member, n)

        hidden_out = share(hidden.astype(BF))

        upstream = upstream_low[:rows].astype(F32)
        results = [None] * LAYERS
        for layer in reversed(range(LAYERS)):
            weights, _ = held[layer]
            unit_low, own_unit, own_inverse, stored = kept[layer]
            mixed, grads, sums, slice_sums = layer_backward(
                upstream_low, unit_low, weights, stored, tables
            )
            bias_sum = jnp.sum(upstream, axis=0, keepdims=True)
            reduced = reduce_tokens(*mixed)
            upstream = upstream + own_inverse * (
                reduced
                - jnp.mean(reduced, axis=-1, keepdims=True)
                - own_unit * jnp.mean(reduced * own_unit, axis=-1, keepdims=True)
            )
            if layer > 0:
                upstream_low = spread_tokens(upstream.astype(BF))
            big = []
            for keep, send in grads:
                own = scatter_rows(keep, send, n).astype(BF)
                big.append((own, pair_swap(own)))
            sums = jnp.concatenate([sums, bias_sum], axis=0)
            sums = sums + tp_swap(sums)
            sums = sums + pair_swap(sums)
            sums = scatter_columns(sums, n)
            slice_sums = sum_fsdp(slice_sums[None], n)
            slice_sums = (slice_sums, pair_swap(slice_sums))
            results[layer] = (big, sums, slice_sums)

        grad_input = share(upstream.astype(BF)).astype(F32)

        def ordered(two):
            own, other = two
            return jnp.where(bit == 0, own, other), jnp.where(bit == 0, other, own)

        outputs = [[] for _ in range(12)]
        for layer in range(LAYERS):
            big, sums, slice_sums = results[layer]
            wide, qkv = [ordered(two) for two in big]
            up = [part[:, :units] for part in wide]
            down = [part[:, units : 2 * units] for part in wide]
            dense = [part[:, 2 * units :] for part in wide]
            outputs[0].append(sums[0])
            outputs[1].append(sums[1])
            outputs[2].append(
                jnp.concatenate(
                    [jnp.swapaxes(part.reshape(-1, 3, width), 0, 1) for part in qkv], axis=2
                ).astype(F32)
            )
            first, second = ordered(slice_sums)
            both = jnp.stack([first[0], second[0]])
            qkv_sums = jnp.swapaxes(both[:, units:].reshape(2, 3, width), 0, 1).reshape(3, -1)
            outputs[3].append(
                lax.dynamic_slice_in_dim(qkv_sums, member * qkv_chunk, qkv_chunk, 1)
            )
            outputs[4].append(jnp.concatenate([part.T for part in dense], axis=0).astype(F32))
            outputs[5].append(sums[4])
            outputs[6].append(sums[2])
            outputs[7].append(sums[3])
            outputs[8].append(jnp.concatenate(up, axis=1).astype(F32))
            outputs[9].append(
                lax.dynamic_slice_in_dim(
                    both[:, :units].reshape(-1), member * up_chunk, up_chunk, 0
                )
            )
            outputs[10].append(jnp.concatenate([part.T for part in down], axis=0).astype(F32))
            outputs[11].append(sums[4])
        return (hidden_out[None], grad_input[None]) + tuple(jnp.stack(out) for out in outputs)

    return on_device


def solution(mesh):
    return jax.shard_map(
        make_body(mesh.shape["fsdp"]),
        mesh=mesh,
        in_specs=(
            P("fsdp", "ctx", None),
            P("fsdp", "ctx", None),
            P("fsdp", None),
            P(None, "fsdp"),
            P(None, "fsdp"),
            P(None, None, "fsdp", "tp"),
            P(None, None, ("tp", "fsdp")),
            P(None, "tp", "fsdp"),
            P(None, "fsdp"),
            P(None, "fsdp"),
            P(None, "fsdp"),
            P(None, "fsdp", "tp"),
            P(None, ("tp", "fsdp")),
            P(None, "tp", "fsdp"),
            P(None, "fsdp"),
        ),
        out_specs=(
            P("fsdp", "ctx", None),
            P("fsdp", "ctx", None),
            P(None, "fsdp"),
            P(None, "fsdp"),
            P(None, None, "fsdp", "tp"),
            P(None, None, ("tp", "fsdp")),
            P(None, "tp", "fsdp"),
            P(None, "fsdp"),
            P(None, "fsdp"),
            P(None, "fsdp"),
            P(None, "fsdp", "tp"),
            P(None, ("tp", "fsdp")),
            P(None, "tp", "fsdp"),
            P(None, "fsdp"),
        ),
        check_vma=False,
    )
```
